32 devices in a mesh: row: 2 (over y), col: 16 (over z, x, core).
Axes of the slice: x: 2, y: 2, z: 4, core: 2. Of those that a mesh axis runs over, the one named last changes fastest.
Arguments:
- tokens: bfloat16 [16384, 1152], P(('col', 'row')), may hold values from -6 to 6
- labels: int32 [64], P('col'), may hold values from 0 to 999
- timesteps: int32 [64], P('col'), may hold values from 0 to 999
- class_table: bfloat16 [1000, 1152], replicated, may hold values from -6 to 6
- ada_weight: bfloat16 [1152, 6912], P('col', 'row'), may hold values from -0.1875 to 0.1875
- ada_bias: bfloat16 [6912], P(('row', 'col')), may hold values from -3 to 3
- qkv_weight: bfloat16 [3, 1152, 1152], P(None, 'col', 'row'), may hold values from -0.1875 to 0.1875
- qkv_bias: bfloat16 [2304], P(('row', 'col')), may hold values from -3 to 3
- proj_weight: bfloat16 [1152, 1152], P('row', 'col'), may hold values from -0.75 to 0.75
- proj_bias: bfloat16 [1152], P('col'), may hold values from -3 to 3
- up_weight: bfloat16 [1152, 4608], P('col', 'row'), may hold values from -0.1875 to 0.1875
- up_bias: bfloat16 [4608], P(('row', 'col')), may hold values from -3 to 3
- down_weight: bfloat16 [4608, 1152], P('row', 'col'), may hold values from -0.09375 to 0.09375
- down_bias: bfloat16 [1152], P('col'), may hold values from -3 to 3
- cotangent: bfloat16 [16384, 1152], P(('col', 'row')), may hold values from -6 to 6
Outputs:
- block_out: bfloat16 [16384, 1152], P(('col', 'row'))
- tokens_grad: float32 [16384, 1152], P(('col', 'row'))
- cond_grad: float32 [64, 1152], P('col', 'row')
- ada_weight_grad: float32 [1152, 6912], P('col', 'row')
- ada_bias_grad: float32 [6912], P(('row', 'col'))
- qkv_weight_grad: float32 [3, 1152, 1152], P(None, 'col', 'row')
- qkv_bias_grad: float32 [2304], P(('row', 'col'))
- proj_weight_grad: float32 [1152, 1152], P('row', 'col')
- proj_bias_grad: float32 [1152], P('col')
- up_weight_grad: float32 [1152, 4608], P('col', 'row')
- up_bias_grad: float32 [4608], P(('row', 'col'))
- down_weight_grad: float32 [4608, 1152], P('row', 'col')
- down_bias_grad: float32 [1152], P('col')
The draws below stay inside these ranges and needn't reach their ends.
All inputs are finite; a program needn't handle non-finite values.
Results may differ from the reference program's by a relative error of at most 0.02.
Values may be sent and summed in bfloat16 or wider, within the bound.
A program may use at most 256 MiB of HBM per device.

```python
import math
import jax
import jax.numpy as jnp
from jax import lax

D = 1152
H = 16
HD = 72
FF = 4608
NCLS = 1000
SEQ = 256
LAT_DEV = 4
LAT = 64


def set_ends(array, key, smallest, high):
    longest = array.shape.index(max(array.shape))
    spots = []
    for shift in (0, 1):
        where = [jax.random.randint(jax.random.fold_in(key, axis), (), 0, length) for axis, length in enumerate(array.shape)]
        where[longest] = (where[longest] + shift) % array.shape[longest]
        spots.append(tuple(where))
    return array.at[spots[0]].set(smallest).at[spots[1]].set(high)


def block_scale(key, dims, split, smallest, largest):
    def one(position, blocks):
        draws = jax.random.uniform(jax.random.fold_in(jax.random.fold_in(key, 6), position), (blocks,), jnp.float32, smallest / len(split), largest / len(split))
        return jnp.repeat(jnp.exp(draws), dims[position] // blocks).reshape((-1,) + (1,) * (len(dims) - position - 1))

    level = one(*split[0])
    for cut in split[1:]:
        level = level * one(*cut)
    return level


def gaussian(rng, extent, scale, bound, pieces=(), kind=jnp.bfloat16):
    array = jax.random.normal(rng, extent, jnp.float32) * scale
    if len(pieces) > 0:
        array = block_scale(rng, extent, pieces, -0.22, 0.18) * array
    return jnp.clip(array, min=-bound, max=bound).astype(kind)


def setup_inputs(seed: int = 0) -> dict:
    key_of = jax.random.split(jax.random.key(seed), 16)
    return {
        "tokens": gaussian(key_of[0], (LAT * SEQ, D), 1.0, 6.0, ((0, 32),)),
        "labels": set_ends(jax.random.randint(key_of[1], (LAT,), 0, NCLS), jax.random.fold_in(key_of[1], 1), 0, NCLS - 1).astype(jnp.int32),
        "timesteps": set_ends(jax.random.randint(key_of[2], (LAT,), 0, 1000), jax.random.fold_in(key_of[2], 1), 0, 999).astype(jnp.int32),
        "class_table": gaussian(key_of[3], (NCLS, D), 1.0, 6.0),
        "ada_weight": gaussian(key_of[4], (D, 6 * D), D ** -0.5, 0.1875, ((0, 16), (1, 2))),
        "ada_bias": gaussian(key_of[5], (6 * D,), 0.5, 3.0, ((0, 32),)),
        "qkv_weight": gaussian(key_of[6], (3, D, D), D ** -0.5, 0.1875, ((1, 16), (2, 2))),
        "qkv_bias": gaussian(key_of[7], (2 * D,), 0.5, 3.0, ((0, 32),)),
        "proj_weight": gaussian(key_of[8], (D, D), (D // 16) ** -0.5, 0.75, ((0, 2), (1, 16))),
        "proj_bias": gaussian(key_of[9], (D,), 0.5, 3.0, ((0, 16),)),
        "up_weight": gaussian(key_of[10], (D, FF), D ** -0.5, 0.1875, ((0, 16), (1, 2))),
        "up_bias": gaussian(key_of[11], (FF,), 0.5, 3.0, ((0, 32),)),
        "down_weight": gaussian(key_of[12], (FF, D), FF ** -0.5, 0.09375, ((0, 2), (1, 16))),
        "down_bias": gaussian(key_of[13], (D,), 0.5, 3.0, ((0, 16),)),
        "cotangent": gaussian(key_of[14], (LAT * SEQ, D), 1.0, 6.0, ((0, 32),)),
    }


EPS = 1e-06
GELU_K = math.sqrt(2.0 / math.pi)
GELU_C = 0.044715

def condition(labels, timesteps, class_table):
    classes = jnp.arange(class_table.shape[0], dtype=jnp.int32)
    onehot = (labels[:, None] == classes[None, :]).astype(jnp.bfloat16)
    embedded = jnp.dot(onehot, class_table, preferred_element_type=jnp.float32)
    half_width = class_table.shape[1] // 2
    frequencies = jnp.exp(-math.log(10000.0) * jnp.arange(half_width, dtype=jnp.float32) / half_width)
    angles = timesteps.astype(jnp.float32)[:, None] * frequencies[None, :]
    return embedded + jnp.concatenate([jnp.cos(angles), jnp.sin(angles)], axis=1)

def normalize(values):
    row_mean = lax.optimization_barrier(jnp.mean(values, axis=-1, keepdims=True))
    centred = values - row_mean
    inv_std = lax.rsqrt(lax.optimization_barrier(jnp.mean(centred * centred, axis=-1, keepdims=True)) + EPS)
    return (centred * inv_std, inv_std)

def normalize_back(normed, inv_std, upstream):
    return inv_std * (upstream - lax.optimization_barrier(jnp.mean(upstream, axis=-1, keepdims=True)) - normed * lax.optimization_barrier(jnp.mean(upstream * normed, axis=-1, keepdims=True)))

def gelu_pair(inputs):
    tanh_part = jnp.tanh(GELU_K * (inputs + GELU_C * inputs * inputs * inputs))
    values = 0.5 * inputs * (1.0 + tanh_part)
    slopes = 0.5 * (1.0 + tanh_part) + 0.5 * inputs * (1.0 - tanh_part * tanh_part) * GELU_K * (1.0 + 3.0 * GELU_C * inputs * inputs)
    return (values, slopes)

def contract_rows(left, right):
    return lax.dot_general(left, right, (((0,), (0,)), ((), ())), preferred_element_type=jnp.float32)

def contract_cols(left, right):
    return lax.dot_general(left, right, (((1,), (1,)), ((), ())), preferred_element_type=jnp.float32)

def rounded(values):
    return lax.optimization_barrier(values.astype(jnp.bfloat16)).astype(jnp.float32)

def attend(queries, key_rows, value_rows, heads, latents):
    head_shape = (latents, SEQ, heads, HD)
    inv_root = 1.0 / math.sqrt(HD)
    query_heads = queries.astype(jnp.float32).reshape(head_shape)
    key_heads = key_rows.astype(jnp.float32).reshape(head_shape)
    value_heads = value_rows.astype(jnp.float32).reshape(head_shape)
    scores = jnp.einsum('lqhe,lkhe->lhqk', query_heads, key_heads) * inv_root
    top_score = lax.optimization_barrier(jnp.max(scores, axis=-1, keepdims=True))
    unnormed = jnp.exp(scores - top_score)
    totals = lax.optimization_barrier(jnp.sum(unnormed, axis=-1, keepdims=True))
    logsum = top_score + jnp.log(totals)
    attn_probs = (unnormed / totals).astype(jnp.bfloat16)
    attended = jnp.einsum('lhqk,lkhe->lqhe', attn_probs.astype(jnp.float32), value_heads).astype(jnp.bfloat16)
    return (attended.reshape(queries.shape), logsum)

def attend_back(queries, key_rows, value_rows, logsum, upstream, heads, latents):
    head_shape = (latents, SEQ, heads, HD)
    inv_root = 1.0 / math.sqrt(HD)
    query_heads = queries.astype(jnp.float32).reshape(head_shape)
    key_heads = key_rows.astype(jnp.float32).reshape(head_shape)
    value_heads = value_rows.astype(jnp.float32).reshape(head_shape)
    upstream_heads = upstream.astype(jnp.float32).reshape(head_shape)
    scores = jnp.einsum('lqhe,lkhe->lhqk', query_heads, key_heads) * inv_root
    attn_probs = jnp.exp(scores - logsum)
    probs_low = attn_probs.astype(jnp.bfloat16).astype(jnp.float32)
    grad_values = jnp.einsum('lhqk,lqhe->lkhe', probs_low, upstream_heads).astype(jnp.bfloat16)
    grad_probs = jnp.einsum('lqhe,lkhe->lhqk', upstream_heads, value_heads)
    row_inner = lax.optimization_barrier(jnp.sum(attn_probs * grad_probs, axis=-1, keepdims=True))
    grad_scores = (attn_probs * (grad_probs - row_inner) * inv_root).astype(jnp.bfloat16).astype(jnp.float32)
    grad_query = jnp.einsum('lhqk,lkhe->lqhe', grad_scores, key_heads).astype(jnp.bfloat16)
    grad_keys = jnp.einsum('lhqk,lqhe->lkhe', grad_scores, query_heads).astype(jnp.bfloat16)
    return (grad_query.reshape(queries.shape), grad_keys.reshape(queries.shape), grad_values.reshape(queries.shape))

def reference(tokens, labels, timesteps, class_table, ada_weight, ada_bias, qkv_weight, qkv_bias, proj_weight, proj_bias, up_weight, up_bias, down_weight, down_bias, cotangent):
    conditioning = condition(labels, timesteps, class_table)
    sigmoid_cond = jax.nn.sigmoid(conditioning)
    activated = (conditioning * sigmoid_cond).astype(jnp.bfloat16)
    modulation = jnp.dot(activated, ada_weight, preferred_element_type=jnp.float32) + ada_bias.astype(jnp.float32)
    bias_pair = qkv_bias.astype(jnp.float32).reshape(H, 2, HD)
    query_bias = bias_pair[:, 0, :].reshape(D)
    value_bias = bias_pair[:, 1, :].reshape(D)
    qkv_wide = qkv_weight.astype(jnp.float32)
    group_size = LAT_DEV
    groups = LAT // group_size
    rows_total = SEQ * group_size

    def per_latent(values):
        return lax.optimization_barrier(jnp.sum(values.reshape(group_size, SEQ, D), axis=1))

    def one_group(totals, inputs):
        source_low, upstream_low, mod_group = inputs
        mod_rows = jnp.repeat(mod_group, SEQ, axis=0)
        parts = [mod_rows[:, block * D:(block + 1) * D] for block in range(6)]
        shift_one, scale_one, gate_one, shift_two, scale_two, gate_two = parts
        source = source_low.astype(jnp.float32)
        normed_one, inv_one = normalize(source)
        flat_one = (normed_one * (1.0 + scale_one) + shift_one).astype(jnp.bfloat16)
        projected = jnp.einsum('nd,kde->nke', flat_one.astype(jnp.float32), qkv_wide)
        queries = (projected[:, 0] + query_bias).astype(jnp.bfloat16)
        key_rows = projected[:, 1].astype(jnp.bfloat16)
        value_rows = (projected[:, 2] + value_bias).astype(jnp.bfloat16)
        flat_att, logsum = attend(queries, key_rows, value_rows, H, group_size)
        attn_out = jnp.dot(flat_att, proj_weight, preferred_element_type=jnp.float32) + proj_bias.astype(jnp.float32)
        middle = source + gate_one * attn_out
        normed_two, inv_two = normalize(middle)
        flat_two = (normed_two * (1.0 + scale_two) + shift_two).astype(jnp.bfloat16)
        pre_act = jnp.dot(flat_two, up_weight, preferred_element_type=jnp.float32) + up_bias.astype(jnp.float32)
        activ_full, slopes = gelu_pair(pre_act)
        activ = activ_full.astype(jnp.bfloat16)
        mlp_out = jnp.dot(activ, down_weight, preferred_element_type=jnp.float32) + down_bias.astype(jnp.float32)
        block_out = (middle + gate_two * mlp_out).astype(jnp.bfloat16)
        upstream = upstream_low.astype(jnp.float32)
        flat_mlp = (gate_two * upstream).astype(jnp.bfloat16)
        grad_pre = (contract_cols(flat_mlp, down_weight) * slopes).astype(jnp.bfloat16)
        grad_hidden_two = contract_cols(grad_pre, up_weight)
        grad_middle = upstream + normalize_back(normed_two, inv_two, grad_hidden_two * (1.0 + scale_two))
        flat_grad_attn = (gate_one * grad_middle).astype(jnp.bfloat16)
        grad_attended = contract_cols(flat_grad_attn, proj_weight).astype(jnp.bfloat16)
        grad_query, grad_keys, grad_values = attend_back(queries, key_rows, value_rows, logsum, grad_attended, H, group_size)
        stacked = jnp.stack([grad_query, grad_keys, grad_values], axis=1)
        stacked_wide = stacked.astype(jnp.float32)
        grad_hidden_one = jnp.einsum('nke,kde->nd', stacked_wide, qkv_wide)
        tokens_grad = grad_middle + normalize_back(normed_one, inv_one, grad_hidden_one * (1.0 + scale_one))
        grad_mod = jnp.concatenate([per_latent(grad_hidden_one), per_latent(grad_hidden_one * normed_one), per_latent(grad_middle * attn_out), per_latent(grad_hidden_two), per_latent(grad_hidden_two * normed_two), per_latent(upstream * mlp_out)], axis=1)
        new_totals = (totals[0] + rounded(jnp.einsum('nd,nke->kde', flat_one.astype(jnp.float32), stacked_wide)), totals[1] + rounded(lax.optimization_barrier(jnp.sum(stacked_wide[:, 0], axis=0))), totals[2] + rounded(lax.optimization_barrier(jnp.sum(stacked_wide[:, 2], axis=0))), totals[3] + rounded(contract_rows(flat_att, flat_grad_attn)), totals[4] + rounded(lax.optimization_barrier(jnp.sum(flat_grad_attn.astype(jnp.float32), axis=0))), totals[5] + rounded(contract_rows(flat_two, grad_pre)), totals[6] + rounded(lax.optimization_barrier(jnp.sum(grad_pre.astype(jnp.float32), axis=0))), totals[7] + rounded(contract_rows(activ, flat_mlp)), totals[8] + rounded(lax.optimization_barrier(jnp.sum(flat_mlp.astype(jnp.float32), axis=0))))
        return (new_totals, (block_out, tokens_grad, grad_mod))
    zeros = (jnp.zeros((3, D, D), jnp.float32), jnp.zeros((D,), jnp.float32), jnp.zeros((D,), jnp.float32), jnp.zeros((D, D), jnp.float32), jnp.zeros((D,), jnp.float32), jnp.zeros((D, FF), jnp.float32), jnp.zeros((FF,), jnp.float32), jnp.zeros((FF, D), jnp.float32), jnp.zeros((D,), jnp.float32))
    inputs = (tokens.reshape(groups, rows_total, D), cotangent.reshape(groups, rows_total, D), modulation.reshape(groups, group_size, 6 * D))
    totals, results = lax.scan(one_group, zeros, inputs)
    outputs, grads_in, grad_mods = results
    grad_modulation = grad_mods.reshape(LAT, 6 * D)
    grad_mod_low = grad_modulation.astype(jnp.bfloat16)

    def ada_group(carry, inputs):
        act_group, mod_group, low_group = inputs
        return ((carry[0] + rounded(contract_rows(act_group, low_group)), carry[1] + rounded(lax.optimization_barrier(jnp.sum(mod_group, axis=0)))), 0)
    ada_inputs = (activated.reshape(groups, group_size, D), grad_mods, grad_mod_low.reshape(groups, group_size, 6 * D))
    ada_totals, unused = lax.scan(ada_group, (jnp.zeros((D, 6 * D), jnp.float32), jnp.zeros((6 * D,), jnp.float32)), ada_inputs)
    ada_weight_grad, ada_bias_grad = ada_totals
    grad_activated = contract_cols(grad_mod_low, ada_weight)
    cond_grad = grad_activated * sigmoid_cond * (1.0 + conditioning * (1.0 - sigmoid_cond))
    qkv_bias_grad = jnp.stack([totals[1].reshape(H, HD), totals[2].reshape(H, HD)], axis=1).reshape(2 * D)
    return (outputs.reshape(LAT * SEQ, D), grads_in.reshape(LAT * SEQ, D), cond_grad, ada_weight_grad, ada_bias_grad, totals[0], qkv_bias_grad, totals[3], totals[4], totals[5], totals[6], totals[7], totals[8])
```

```python
import math

import jax
import jax.numpy as jnp
from jax import lax
from jax.sharding import PartitionSpec as P

D = 1152
HD = 72
SEQ = 256


EPS = 1e-06
GELU_K = math.sqrt(2.0 / math.pi)
GELU_C = 0.044715


def condition(labels, timesteps, class_table):
    classes = jnp.arange(class_table.shape[0], dtype=jnp.int32)
    onehot = (labels[:, None] == classes[None, :]).astype(jnp.bfloat16)
    embedded = jnp.dot(onehot, class_table, preferred_element_type=jnp.float32)
    half_width = class_table.shape[1] // 2
    frequencies = jnp.exp(
        -math.log(10000.0) * jnp.arange(half_width, dtype=jnp.float32) / half_width
    )
    angles = timesteps.astype(jnp.float32)[:, None] * frequencies[None, :]
    return embedded + jnp.concatenate([jnp.cos(angles), jnp.sin(angles)], axis=1)


def normalize(values):
    row_mean = jnp.mean(values, axis=-1, keepdims=True)
    centred = values - row_mean
    inv_std = lax.rsqrt(jnp.mean(centred * centred, axis=-1, keepdims=True) + EPS)
    return (centred * inv_std, inv_std)


def normalize_back(normed, inv_std, upstream):
    return inv_std * (
        upstream
        - jnp.mean(upstream, axis=-1, keepdims=True)
        - normed * jnp.mean(upstream * normed, axis=-1, keepdims=True)
    )


def gelu_pair(inputs):
    tanh_part = jnp.tanh(GELU_K * (inputs + GELU_C * inputs * inputs * inputs))
    values = 0.5 * inputs * (1.0 + tanh_part)
    slopes = 0.5 * (1.0 + tanh_part) + 0.5 * inputs * (1.0 - tanh_part * tanh_part) * GELU_K * (
        1.0 + 3.0 * GELU_C * inputs * inputs
    )
    return (values, slopes)


def contract_rows(left, right):
    return lax.dot_general(
        left, right, (((0,), (0,)), ((), ())), preferred_element_type=jnp.float32
    )


def contract_cols(left, right):
    return lax.dot_general(
        left, right, (((1,), (1,)), ((), ())), preferred_element_type=jnp.float32
    )


def contract_cross(left, right):
    return lax.dot_general(
        left, right, (((0,), (1,)), ((), ())), preferred_element_type=jnp.float32
    )


def exact_rows(left, right):
    return lax.dot_general(
        left,
        right,
        (((0,), (0,)), ((), ())),
        precision=lax.Precision.HIGHEST,
        preferred_element_type=jnp.float32,
    )


def attend(query_cols, key_cols, value_cols, heads, latents):
    head_shape = (heads, HD, latents, SEQ)
    inv_root = 1.0 / math.sqrt(HD)
    query_heads = query_cols.reshape(head_shape)
    key_heads = key_cols.reshape(head_shape)
    value_heads = value_cols.reshape(head_shape)
    scores = (
        jnp.einsum("hels,helt->lhst", query_heads, key_heads, preferred_element_type=jnp.float32)
        * inv_root
    )
    top_score = jnp.max(scores, axis=-1, keepdims=True)
    unnormed = jnp.exp(scores - top_score)
    totals = jnp.sum(unnormed, axis=-1, keepdims=True)
    logsum = top_score + jnp.log(totals)
    attn_probs = (unnormed / totals).astype(jnp.bfloat16)
    attended = jnp.einsum(
        "lhst,helt->hels", attn_probs, value_heads, preferred_element_type=jnp.float32
    ).astype(jnp.bfloat16)
    return (attended.reshape(query_cols.shape), logsum)


def attend_back(query_cols, key_cols, value_cols, logsum, upstream_cols, heads, latents):
    head_shape = (heads, HD, latents, SEQ)
    inv_root = 1.0 / math.sqrt(HD)
    query_heads = query_cols.reshape(head_shape)
    key_heads = key_cols.reshape(head_shape)
    value_heads = value_cols.reshape(head_shape)
    upstream_heads = upstream_cols.reshape(head_shape)
    scores = (
        jnp.einsum("hels,helt->lhst", query_heads, key_heads, preferred_element_type=jnp.float32)
        * inv_root
    )
    attn_probs = jnp.exp(scores - logsum)
    probs_low = attn_probs.astype(jnp.bfloat16)
    grad_values = jnp.einsum(
        "lhst,hels->helt", probs_low, upstream_heads, preferred_element_type=jnp.float32
    ).astype(jnp.bfloat16)
    grad_probs = jnp.einsum(
        "hels,helt->lhst", upstream_heads, value_heads, preferred_element_type=jnp.float32
    )
    row_inner = jnp.sum(attn_probs * grad_probs, axis=-1, keepdims=True)
    grad_scores = (attn_probs * (grad_probs - row_inner) * inv_root).astype(jnp.bfloat16)
    grad_query = jnp.einsum(
        "lhst,helt->hels", grad_scores, key_heads, preferred_element_type=jnp.float32
    ).astype(jnp.bfloat16)
    grad_keys = jnp.einsum(
        "lhst,hels->helt", grad_scores, query_heads, preferred_element_type=jnp.float32
    ).astype(jnp.bfloat16)
    return (
        grad_query.reshape(query_cols.shape),
        grad_keys.reshape(query_cols.shape),
        grad_values.reshape(query_cols.shape),
    )


def local(
    tokens,
    labels,
    timesteps,
    class_table,
    ada_weight,
    ada_bias,
    qkv_weight,
    qkv_bias,
    proj_weight,
    proj_bias,
    up_weight,
    up_bias,
    down_weight,
    down_bias,
    cotangent,
):
    local_rows = tokens.shape[0]
    latents = labels.shape[0]
    row_devices = lax.axis_size("row")
    gathered = (
        lax.all_gather(ada_weight, "col", axis=0, tiled=True),
        lax.all_gather(ada_bias, "col", axis=0, tiled=True),
        lax.all_gather(qkv_weight, "col", axis=1, tiled=True),
        lax.all_gather(qkv_bias, "col", axis=0, tiled=True),
        lax.all_gather(proj_weight, "col", axis=1, tiled=True),
        lax.all_gather(proj_bias, "col", axis=0, tiled=True),
        lax.all_gather(up_weight, "col", axis=0, tiled=True),
        lax.all_gather(up_bias, "col", axis=0, tiled=True),
        lax.all_gather(down_weight, "col", axis=1, tiled=True),
        lax.all_gather(down_bias, "col", axis=0, tiled=True),
    )
    (
        ada_full,
        ada_bias_full,
        qkv_full,
        qkv_bias_full,
        proj_full,
        proj_bias_full,
        up_full,
        up_bias_full,
        down_full,
        down_bias_full,
    ) = gathered
    local_width = qkv_full.shape[2]
    local_heads = local_width // HD
    row_latent = (
        lax.axis_index("row") * local_rows + jnp.arange(local_rows, dtype=jnp.int32)
    ) // SEQ
    picker = (row_latent[:, None] == jnp.arange(latents, dtype=jnp.int32)[None, :]).astype(
        jnp.float32
    )
    conditioning = condition(labels, timesteps, class_table)
    sigmoid_cond = jax.nn.sigmoid(conditioning)
    activated = (conditioning * sigmoid_cond).astype(jnp.bfloat16)
    partial_mod = jnp.dot(
        activated, ada_full, preferred_element_type=jnp.float32
    ) + ada_bias_full.astype(jnp.float32)
    modulation = lax.all_gather(partial_mod, "row", axis=1, tiled=True)
    mod_rows = jnp.dot(
        picker, modulation, precision=lax.Precision.HIGHEST, preferred_element_type=jnp.float32
    )
    parts = [mod_rows[:, block * D : (block + 1) * D] for block in range(6)]
    shift_one, scale_one, gate_one, shift_two, scale_two, gate_two = parts
    source = tokens.astype(jnp.float32)
    normed_one, inv_one = normalize(source)
    hidden_one = (normed_one * (1.0 + scale_one) + shift_one).astype(jnp.bfloat16)
    flat_one = lax.all_gather(hidden_one, "row", axis=0, tiled=True)
    bias_pair = qkv_bias_full.astype(jnp.float32).reshape(local_heads, 2, HD)
    query_bias = bias_pair[:, 0].reshape(local_width, 1)
    value_bias = bias_pair[:, 1].reshape(local_width, 1)
    query_cols = (contract_cross(qkv_full[0], flat_one) + query_bias).astype(jnp.bfloat16)
    key_cols = contract_cross(qkv_full[1], flat_one).astype(jnp.bfloat16)
    value_cols = (contract_cross(qkv_full[2], flat_one) + value_bias).astype(jnp.bfloat16)
    attended, logsum = attend(query_cols, key_cols, value_cols, local_heads, latents)
    piece = attended
    attn_out = lax.psum_scatter(
        contract_rows(piece, proj_full).astype(jnp.bfloat16), "row", scatter_dimension=0, tiled=True
    ).astype(jnp.float32) + proj_bias_full.astype(jnp.float32)
    middle = source + gate_one * attn_out
    normed_two, inv_two = normalize(middle)
    hidden_two = (normed_two * (1.0 + scale_two) + shift_two).astype(jnp.bfloat16)
    flat_two = lax.all_gather(hidden_two, "row", axis=0, tiled=True)
    pre_act = jnp.dot(flat_two, up_full, preferred_element_type=jnp.float32) + up_bias_full.astype(
        jnp.float32
    )
    activ_full, slopes = gelu_pair(pre_act)
    activ = activ_full.astype(jnp.bfloat16)
    piece = activ
    mlp_out = lax.psum_scatter(
        jnp.dot(piece, down_full, preferred_element_type=jnp.float32).astype(jnp.bfloat16),
        "row",
        scatter_dimension=0,
        tiled=True,
    ).astype(jnp.float32) + down_bias_full.astype(jnp.float32)
    block_out = (middle + gate_two * mlp_out).astype(jnp.bfloat16)
    upstream = cotangent.astype(jnp.float32)
    grad_mlp = (gate_two * upstream).astype(jnp.bfloat16)
    flat_mlp = lax.all_gather(grad_mlp, "row", axis=0, tiled=True)
    down_weight_grad = contract_rows(activ, flat_mlp)
    down_bias_grad = jnp.sum(flat_mlp, axis=0, dtype=jnp.float32)
    grad_pre = (contract_cols(flat_mlp, down_full) * slopes).astype(jnp.bfloat16)
    up_weight_grad = contract_rows(flat_two, grad_pre)
    up_bias_grad = jnp.sum(grad_pre, axis=0, dtype=jnp.float32)
    piece = grad_pre
    grad_hidden_two = lax.psum_scatter(
        contract_cols(piece, up_full).astype(jnp.bfloat16), "row", scatter_dimension=0, tiled=True
    ).astype(jnp.float32)
    grad_middle = upstream + normalize_back(
        normed_two, inv_two, grad_hidden_two * (1.0 + scale_two)
    )
    grad_attn = (gate_one * grad_middle).astype(jnp.bfloat16)
    flat_grad_attn = lax.all_gather(grad_attn, "row", axis=0, tiled=True)
    proj_weight_grad = jnp.dot(attended, flat_grad_attn, preferred_element_type=jnp.float32)
    proj_bias_grad = jnp.sum(flat_grad_attn, axis=0, dtype=jnp.float32)
    grad_attended = contract_cols(proj_full, flat_grad_attn).astype(jnp.bfloat16)
    grad_query, grad_keys, grad_values = attend_back(
        query_cols, key_cols, value_cols, logsum, grad_attended, local_heads, latents
    )
    qkv_weight_grad = jnp.stack(
        [
            contract_cross(flat_one, grad_query),
            contract_cross(flat_one, grad_keys),
            contract_cross(flat_one, grad_values),
        ],
        axis=0,
    )
    query_sum = jnp.sum(grad_query, axis=1, dtype=jnp.float32)
    value_sum = jnp.sum(grad_values, axis=1, dtype=jnp.float32)
    qkv_bias_grad = jnp.stack(
        [query_sum.reshape(local_heads, HD), value_sum.reshape(local_heads, HD)], axis=1
    ).reshape(2 * local_width)
    total = jnp.zeros((local_rows * lax.axis_size("row"), D), jnp.float32)
    for which, grads in enumerate((grad_query, grad_keys, grad_values)):
        piece = grads
        total = total + contract_cross(piece, qkv_full[which])
    grad_hidden_one = lax.psum_scatter(
        total.astype(jnp.bfloat16), "row", scatter_dimension=0, tiled=True
    ).astype(jnp.float32)
    tokens_grad = grad_middle + normalize_back(
        normed_one, inv_one, grad_hidden_one * (1.0 + scale_one)
    )
    row_terms = jnp.concatenate(
        [
            grad_hidden_one,
            grad_hidden_one * normed_one,
            grad_middle * attn_out,
            grad_hidden_two,
            grad_hidden_two * normed_two,
            upstream * mlp_out,
        ],
        axis=1,
    )
    grad_mod_part = exact_rows(picker, row_terms)
    grad_modulation = lax.psum_scatter(
        grad_mod_part.astype(jnp.bfloat16), "row", scatter_dimension=1, tiled=True
    ).astype(jnp.float32)
    ada_bias_grad = jnp.sum(grad_modulation, axis=0)
    grad_mod_low = grad_modulation.astype(jnp.bfloat16)
    ada_weight_grad = contract_rows(activated, grad_mod_low)
    grad_act_part = contract_cols(grad_mod_low, ada_full)
    grad_activated = lax.psum_scatter(grad_act_part, "row", scatter_dimension=1, tiled=True)
    slice_width = D // row_devices
    cond_slice = lax.dynamic_slice_in_dim(
        conditioning, lax.axis_index("row") * slice_width, slice_width, 1
    )
    sigmoid_slice = jax.nn.sigmoid(cond_slice)
    cond_grad = grad_activated * sigmoid_slice * (1.0 + cond_slice * (1.0 - sigmoid_slice))
    summed_grads = tuple(
        (
            lax.psum_scatter(
                ada_weight_grad.astype(jnp.bfloat16), "col", scatter_dimension=0, tiled=True
            ).astype(jnp.float32),
            lax.psum_scatter(
                ada_bias_grad.astype(jnp.bfloat16), "col", scatter_dimension=0, tiled=True
            ).astype(jnp.float32),
            lax.psum_scatter(
                qkv_weight_grad.astype(jnp.bfloat16), "col", scatter_dimension=1, tiled=True
            ).astype(jnp.float32),
            lax.psum_scatter(
                qkv_bias_grad.astype(jnp.bfloat16), "col", scatter_dimension=0, tiled=True
            ).astype(jnp.float32),
            lax.psum_scatter(
                proj_weight_grad.astype(jnp.bfloat16), "col", scatter_dimension=1, tiled=True
            ).astype(jnp.float32),
            lax.psum_scatter(
                proj_bias_grad.astype(jnp.bfloat16), "col", scatter_dimension=0, tiled=True
            ).astype(jnp.float32),
            lax.psum_scatter(
                up_weight_grad.astype(jnp.bfloat16), "col", scatter_dimension=0, tiled=True
            ).astype(jnp.float32),
            lax.psum_scatter(
                up_bias_grad.astype(jnp.bfloat16), "col", scatter_dimension=0, tiled=True
            ).astype(jnp.float32),
            lax.psum_scatter(
                down_weight_grad.astype(jnp.bfloat16), "col", scatter_dimension=1, tiled=True
            ).astype(jnp.float32),
            lax.psum_scatter(
                down_bias_grad.astype(jnp.bfloat16), "col", scatter_dimension=0, tiled=True
            ).astype(jnp.float32),
        )
    )
    return (block_out, tokens_grad, cond_grad) + summed_grads


PAIR = ((0, 1), (1, 0))
ALL = ("row", "chip", "core")
COL = ("chip", "core")


def exchange(values, axis="core"):
    return lax.ppermute(values, axis, PAIR)


def both(values):
    return jnp.concatenate([values, exchange(values)], axis=0)


def spread(block):
    moved = lax.ppermute(block, ("row", "core"), ((0, 0), (1, 2), (2, 1), (3, 3)))
    return lax.all_gather(moved, ("chip", "row"), axis=0, tiled=True)


def collect(grad):
    summed = lax.psum_scatter(
        grad.astype(jnp.bfloat16), ("chip", "row"), scatter_dimension=0, tiled=True
    )
    return lax.ppermute(summed, ("row", "core"), ((0, 0), (1, 2), (2, 1), (3, 3))).astype(
        jnp.float32
    )


def paired(
    tokens,
    labels,
    timesteps,
    class_table,
    ada_weight,
    ada_bias,
    qkv_weight,
    qkv_bias,
    proj_weight,
    proj_bias,
    up_weight,
    up_bias,
    down_weight,
    down_bias,
    cotangent,
):
    f32 = jnp.float32
    low = jnp.bfloat16
    rows = tokens.shape[0]
    mine = rows // SEQ
    shared = labels.shape[0]
    row = lax.axis_index("row")
    core = lax.axis_index("core")
    col = lax.axis_index(COL)
    n_row = lax.axis_size("row")
    n_col = lax.axis_size(COL)
    latents = shared * n_col
    k_rows, mod_half = ada_weight.shape

    small = (ada_bias, qkv_bias, up_bias, proj_bias, down_bias, labels, timesteps)
    packed = jnp.concatenate([v.astype(f32) for v in small])
    used = packed.shape[0]
    packed = jnp.pad(packed, (0, -used % 1024)).reshape(-1, 128)
    fetched = lax.all_gather(packed, ALL, axis=0, tiled=False).reshape(n_row, n_col, -1)
    pieces = []
    start = 0
    for v in small:
        pieces.append(fetched[:, :, start : start + v.shape[0]])
        start += v.shape[0]
    ada_bias_full = pieces[0].reshape(-1)
    qkv_bias_half = lax.dynamic_index_in_dim(pieces[1], core, 0, False).reshape(-1)
    up_bias_half = lax.dynamic_index_in_dim(pieces[2], core, 0, False).reshape(-1)
    proj_bias_full = pieces[3][0].reshape(-1)
    down_bias_full = pieces[4][0].reshape(-1)
    all_labels = pieces[5][0].reshape(-1).astype(jnp.int32)
    all_steps = pieces[6][0].reshape(-1).astype(jnp.int32)

    width = qkv_weight.shape[2]
    heads = width // HD
    qkv_full = spread(qkv_weight.transpose(1, 0, 2).reshape(k_rows, 3 * width))
    proj_full = spread(proj_weight.T)
    up_full = spread(up_weight)
    down_full = spread(down_weight.T)

    conditioning = condition(all_labels, all_steps, class_table)
    activated = (conditioning * jax.nn.sigmoid(conditioning)).astype(low)
    act_block = lax.dynamic_slice_in_dim(activated, col * k_rows, k_rows, 1)
    mod_part = jnp.dot(act_block, ada_weight, preferred_element_type=f32)
    mod_some = lax.psum_scatter(
        mod_part.reshape(n_col, shared, mod_half), COL, scatter_dimension=0, tiled=False
    )
    mod_mine = lax.dynamic_slice_in_dim(mod_some, row * mine, mine, 0)
    mod_theirs = lax.dynamic_slice_in_dim(mod_some, (1 - row) * mine, mine, 0)
    mod_came = exchange(mod_theirs, "row")
    modulation = (
        jnp.concatenate(
            [jnp.where(row == 0, mod_mine, mod_came), jnp.where(row == 0, mod_came, mod_mine)],
            axis=1,
        )
        + ada_bias_full
    )
    parts = [modulation[:, None, block * D : (block + 1) * D] for block in range(6)]
    shift_one, scale_one, gate_one, shift_two, scale_two, gate_two = parts

    def tall(values):
        return values.reshape(mine, SEQ, D)

    def flat(values):
        return values.reshape(rows, D)

    upstream = tall(cotangent).astype(f32)
    grad_mlp = flat((gate_two * upstream).astype(low))
    flat_mlp = both(grad_mlp)

    source = tall(tokens).astype(f32)
    normed_one, inv_one = normalize(source)
    hidden_one = flat((normed_one * (1.0 + scale_one) + shift_one).astype(low))
    flat_one = both(hidden_one)
    bias_pair = qkv_bias_half.reshape(heads, 2, HD)
    bias_col = jnp.concatenate(
        [bias_pair[:, 0].reshape(width), jnp.zeros((width,), f32), bias_pair[:, 1].reshape(width)]
    ).reshape(3 * width, 1)
    qkv_cols = (contract_cross(qkv_full, flat_one) + bias_col).astype(low)
    query_cols = qkv_cols[:width]
    key_cols = qkv_cols[width : 2 * width]
    value_cols = qkv_cols[2 * width :]
    attended, logsum = attend(query_cols, key_cols, value_cols, heads, shared)
    there = exchange(contract_cross(attended[:, rows:], proj_full).astype(low))
    here = contract_cross(attended[:, :rows], proj_full)
    attn_out = tall(here + there.astype(f32) + proj_bias_full)
    middle = source + gate_one * attn_out
    normed_two, inv_two = normalize(middle)
    hidden_two = flat((normed_two * (1.0 + scale_two) + shift_two).astype(low))
    flat_two = both(hidden_two)
    pre_act = jnp.dot(flat_two, up_full, preferred_element_type=f32) + up_bias_half
    activ_full, slopes = gelu_pair(pre_act)
    activ = activ_full.astype(low)
    down_grad = collect(contract_rows(flat_mlp, activ)).T
    grad_pre = (jnp.dot(flat_mlp, down_full, preferred_element_type=f32) * slopes).astype(low)
    there = exchange(contract_cols(grad_pre[rows:], up_full).astype(low))
    here = contract_cols(grad_pre[:rows], up_full)
    grad_hidden_two = tall(here + there.astype(f32))
    up_grad = collect(contract_rows(flat_two, grad_pre))
    there = exchange(contract_cols(activ[rows:], down_full).astype(low))
    here = contract_cols(activ[:rows], down_full)
    mlp_out = tall(here + there.astype(f32) + down_bias_full)
    block_out = flat((middle + gate_two * mlp_out).astype(low))

    grad_middle = upstream + normalize_back(
        normed_two, inv_two, grad_hidden_two * (1.0 + scale_two)
    )
    grad_attn = flat((gate_one * grad_middle).astype(low))
    flat_grad_attn = both(grad_attn)
    grad_attended = contract_cross(proj_full, flat_grad_attn).astype(low)
    grads = jnp.concatenate(
        attend_back(query_cols, key_cols, value_cols, logsum, grad_attended, heads, shared), axis=0
    )
    there = exchange(contract_cross(grads[:, rows:], qkv_full).astype(low))
    here = contract_cross(grads[:, :rows], qkv_full)
    grad_hidden_one = tall(here + there.astype(f32))
    proj_grad = collect(contract_cross(flat_grad_attn, attended)).T
    qkv_grad = (
        collect(contract_cross(flat_one, grads)).reshape(k_rows, 3, width).transpose(1, 0, 2)
    )
    tokens_grad = flat(
        grad_middle
        + normalize_back(normed_one, inv_one, grad_hidden_one * (1.0 + scale_one))
    )

    grad_mod = jnp.concatenate(
        [
            jnp.sum(term, axis=1)
            for term in (
                grad_hidden_one,
                grad_hidden_one * normed_one,
                grad_middle * attn_out,
                grad_hidden_two,
                grad_hidden_two * normed_two,
                upstream * mlp_out,
            )
        ],
        axis=1,
    ).astype(low)
    mod_all = lax.all_gather(grad_mod, COL + ("row",), axis=0, tiled=False)
    mod_all = lax.dynamic_slice_in_dim(mod_all, row * mod_half, mod_half, 2).reshape(
        latents, mod_half
    )
    ada_bias_sum = jnp.sum(mod_all, axis=0, dtype=f32)
    ada_bias_grad = lax.dynamic_slice_in_dim(
        ada_bias_sum, col * ada_bias.shape[0], ada_bias.shape[0], 0
    )
    ada_weight_grad = contract_rows(act_block, mod_all)
    act_part = contract_cols(mod_all, ada_weight)
    act_all = lax.all_gather(act_part, ALL, axis=0, tiled=False).reshape(
        n_row, n_col, latents, k_rows
    )
    slice_blocks = n_col // n_row
    act_mine = lax.dynamic_slice(
        act_all,
        (0, row * slice_blocks, col * shared, 0),
        (n_row, slice_blocks, shared, k_rows),
    )
    grad_activated = (
        jnp.sum(act_mine, axis=0).transpose(1, 0, 2).reshape(shared, slice_blocks * k_rows)
    )
    cond_slice = lax.dynamic_slice(
        conditioning,
        (col * shared, row * slice_blocks * k_rows),
        (shared, slice_blocks * k_rows),
    )
    sigmoid_slice = jax.nn.sigmoid(cond_slice)
    cond_grad = grad_activated * sigmoid_slice * (1.0 + cond_slice * (1.0 - sigmoid_slice))

    sums = jnp.sum(grads, axis=1, dtype=f32)
    qkv_bias_sum = jnp.stack(
        [sums[:width].reshape(heads, HD), sums[2 * width :].reshape(heads, HD)], axis=1
    )
    up_bias_sum = jnp.sum(grad_pre, axis=0, dtype=f32)
    proj_bias_sum = jnp.sum(grad_attn, axis=0, dtype=f32)
    down_bias_sum = jnp.sum(grad_mlp, axis=0, dtype=f32)
    is_half = (jnp.arange(n_row) == core).astype(f32)[:, None, None]

    def halved(values):
        return is_half * values.reshape(1, n_col, -1)

    def repeated(values):
        return jnp.broadcast_to(values.reshape(1, n_col, -1), (n_row, n_col, values.size // n_col))

    sums = jnp.concatenate(
        [
            halved(qkv_bias_sum),
            halved(up_bias_sum),
            repeated(proj_bias_sum),
            repeated(down_bias_sum),
        ],
        axis=2,
    )
    sums = jnp.pad(sums, ((0, 0), (0, 0), (0, -sums.shape[2] % 1024)))
    own = lax.psum_scatter(
        sums.reshape(n_row * n_col, -1, 128), ALL, scatter_dimension=0, tiled=False
    ).reshape(-1)
    bias_grads = []
    start = 0
    for v in (qkv_bias, up_bias, proj_bias, down_bias):
        bias_grads.append(own[start : start + v.shape[0]])
        start += v.shape[0]
    return (
        block_out,
        tokens_grad,
        cond_grad,
        ada_weight_grad,
        ada_bias_grad,
        qkv_grad,
        bias_grads[0],
        proj_grad,
        bias_grads[2],
        up_grad,
        bias_grads[1],
        down_grad,
        bias_grads[3],
    )


def solution(mesh):
    if mesh.shape["row"] == 2 and mesh.shape["col"] % 2 == 0:
        split = jax.sharding.Mesh(
            mesh.devices.reshape(2, mesh.shape["col"] // 2, 2), ("row", "chip", "core")
        )
        assert mesh.axis_names == ("row", "col")
        return over(split, paired, COL)
    return over(mesh, local, ("col",))


def over(mesh, body, col):
    row = ("row",)
    in_specs = (
        P(col + row, None),
        P(col),
        P(col),
        P(),
        P(col, "row"),
        P(row + col),
        P(None, col, "row"),
        P(row + col),
        P("row", col),
        P(col),
        P(col, "row"),
        P(row + col),
        P("row", col),
        P(col),
        P(col + row, None),
    )
    out_specs = (
        P(col + row, None),
        P(col + row, None),
        P(col, "row"),
        P(col, "row"),
        P(row + col),
        P(None, col, "row"),
        P(row + col),
        P("row", col),
        P(col),
        P(col, "row"),
        P(row + col),
        P("row", col),
        P(col),
    )
    return jax.shard_map(body, mesh=mesh, in_specs=in_specs, out_specs=out_specs, check_vma=False)
```
